512 devices in a mesh: row: 32 (over y, x, core), col: 16 (over z).
Axes of the slice: x: 4, y: 4, z: 16, core: 2. Of those that a mesh axis runs over, the one named last changes fastest.
Arguments:
- a_tile: bfloat16 [8192, 16384], P('row', 'col'), may hold values from -6 to 6
- b_tile: bfloat16 [16384, 26624], P('row', 'col'), may hold values from -0.046875 to 0.046875
- c_prior: bfloat16 [8192, 26624], P('row', 'col'), may hold values from -0.29882812 to 0.29882812
- sketch_matrix: bfloat16 [26624, 128], P('col'), may hold values from -0.0390625 to 0.0390625
- panel_ids: int32 [2], replicated, may hold values from 0 to 31
Outputs:
- c_out: bfloat16 [8192, 26624], P('row', 'col')
- sketch: float32 [8192, 128], P('row')
- predicted: float32 [8192, 128], P('row')
The draws below stay inside these ranges and needn't reach their ends.
Inputs may be any that keep to these rules, and one draw needn't show every extreme that they name: `panel_ids`: the 2 ids may repeat.
All inputs are finite; a program needn't handle non-finite values.
Results may differ from the reference program's by a relative error of at most 0.0029.
Values may be sent and summed in bfloat16 or wider, within the bound.
A program may use at most 64 MiB of HBM per device.

```python
import jax
import jax.numpy as jnp
from jax import lax

K = 16384
FF_W = 26624
PANEL = 512
STEPS = 2
SK = 128
TOKENS = 8192


def shard_levels(stream_key, dims, pieces, least, top_value):
    loudness = 1.0
    for dim, blocks in pieces:
        heights = jax.random.uniform(jax.random.fold_in(jax.random.fold_in(stream_key, 6), dim), (blocks,), jnp.float32, least / len(pieces), top_value / len(pieces))
        loudness = loudness * jnp.repeat(jnp.exp(heights), dims[dim] // blocks).reshape((-1,) + (1,) * (len(dims) - 1 - dim))
    return loudness


def normal_values(rng, extent, deviation, reach, split=(), held_as=jnp.bfloat16):
    drawn = jax.random.normal(rng, extent, jnp.float32) * deviation
    if len(split) > 0:
        drawn = shard_levels(rng, extent, split, -0.22, 0.18) * drawn
    return jnp.clip(drawn, min=-reach, max=reach).astype(held_as)


def setup_inputs(seed: int = 0) -> dict:
    key_of = jax.random.split(jax.random.key(seed), 6)
    a_tile = normal_values(key_of[0], (TOKENS, K), 1.0, 6.0, ((0, 32), (1, 16)))
    b_tile = normal_values(key_of[1], (K, FF_W), K ** -0.5, 0.046875, ((0, 32), (1, 16)))
    c_prior = normal_values(key_of[2], (TOKENS, FF_W), 0.05, 0.29882812, ((0, 32), (1, 16)))
    sketch_matrix = normal_values(key_of[3], (FF_W, SK), FF_W ** -0.5, 0.0390625, ((0, 16),))
    panel_ids = jax.random.randint(key_of[4], (STEPS,), 0, K // PANEL).astype(jnp.int32)
    return dict(a_tile=a_tile, b_tile=b_tile, c_prior=c_prior, sketch_matrix=sketch_matrix, panel_ids=panel_ids)


def reference(a_tile, b_tile, c_prior, sketch_matrix, panel_ids):
    running = c_prior.astype(jnp.float32)
    predicted = jnp.zeros((a_tile.shape[0], sketch_matrix.shape[1]), jnp.float32)
    for step in range(STEPS):
        first_row = (panel_ids[step] * PANEL).astype(jnp.int32)
        a_panel = lax.dynamic_slice_in_dim(a_tile, first_row, PANEL, 1)
        b_panel = lax.dynamic_slice_in_dim(b_tile, first_row, PANEL, 0)
        running = running + jnp.dot(a_panel, b_panel, preferred_element_type=jnp.float32)
        panel_sketch = jnp.dot(b_panel, sketch_matrix, preferred_element_type=jnp.float32)
        predicted = predicted + jnp.dot(a_panel.astype(jnp.float32), panel_sketch, precision=lax.Precision.HIGHEST)
    c_out = running.astype(jnp.bfloat16)
    sketch = jnp.dot(c_out, sketch_matrix, preferred_element_type=jnp.float32)
    return c_out, sketch, predicted
```

```python
import functools

import jax
import jax.numpy as jnp
from jax import lax
from jax.experimental import pallas as pl
from jax.experimental.pallas import tpu as pltpu
from jax.sharding import PartitionSpec as P

PANEL = 512
STEPS = 2
NX = 4
NY = 4
LANE = 128
DELAY = 3
MESH = pl.DeviceIdType.MESH


def kernel(dims, ids, a_hbm, b_hbm, c_hbm, s_hbm, cout_hbm, sk_hbm, pr_hbm,
           a_v, bo_v, bp_v, c_v, s_v, sbuf, recv, precv, afull, bfull, cov,
           part, rsr, red, outb, bs, masks,
           bo_sem, bp_send, bp_recv, in_sem, send_sem, recv_sem, f_send, f_recv,
           rs_sem, out_sem):
    nz, ncol, nblk, total, rows_b, rows_k = dims
    seg = 2 * rows_b
    r = lax.axis_index("row")
    z = lax.axis_index("col")
    core = lax.rem(r, 2)
    chip = r // 2
    x = lax.rem(chip, NX)
    y = chip // NX

    def at_chip(yy, xx):
        return (lax.rem(yy + NY, NY) * NX + lax.rem(xx + NX, NX)) * 2 + core

    partner = (chip * 2 + (1 - core), z)
    links = (
        (at_chip(y, x + 1), z), (at_chip(y, x - 1), z),
        (at_chip(y + 1, x), z), (at_chip(y - 1, x), z),
        (r, lax.rem(z + 1, nz)), (r, lax.rem(z + nz - 1, nz)),
    )
    half = PANEL // 2
    mine = pl.multiple_of(core * half, half)
    other = pl.multiple_of((1 - core) * half, half)

    def own_load(j, k):
        rows = mine if j == 0 else other
        return pltpu.make_async_copy(
            b_hbm.at[pl.ds(rows, half), pl.ds(pl.multiple_of(k * LANE, LANE), LANE)],
            bo_v.at[k, pl.ds(rows, half), :], bo_sem.at[j, k])

    def partner_copy(j, k):
        rows = other if j == 0 else mine
        return pltpu.make_async_remote_copy(
            src_ref=b_hbm.at[pl.ds(rows, half), pl.ds(pl.multiple_of(k * LANE, LANE), LANE)],
            dst_ref=bp_v.at[k, pl.ds(rows, half), :],
            send_sem=bp_send.at[j, k], recv_sem=bp_recv.at[j, k],
            device_id=partner, device_id_type=MESH)

    load_a = pltpu.make_async_copy(a_hbm, a_v, in_sem.at[0])
    load_c = pltpu.make_async_copy(c_hbm, c_v, in_sem.at[1])
    load_s = pltpu.make_async_copy(s_hbm, s_v, in_sem.at[2])

    barrier = pltpu.get_barrier_semaphore()
    for target in links + (partner,):
        pl.semaphore_signal(barrier, inc=1, device_id=target, device_id_type=MESH)
    load_a.start()
    for k in range(nblk):
        own_load(0, k).start()
    pl.semaphore_wait(barrier, 7)
    for k in range(nblk):
        partner_copy(0, k).start()
    load_c.start()
    load_s.start()
    for k in range(nblk):
        own_load(1, k).start()
        partner_copy(1, k).start()
    load_a.wait()

    def flag(cond):
        return cond.astype(jnp.int32)

    def choose(cond, one, two):
        return two + cond * (one - two)

    def within(v, low, high):
        return flag(v >= low) * flag(v <= high)

    pid = [ids[s] for s in range(STEPS)]
    owner_core = [lax.rem(p, 2) for p in pid]
    ox = [lax.rem(lax.div(p, 2), NX) for p in pid]
    oy = [lax.div(p, 2 * NX) for p in pid]
    oz = [lax.div(p * PANEL, rows_k) for p in pid]
    oa = [lax.rem(p * PANEL, rows_k) for p in pid]
    dx = [lax.rem(x - o + NX, NX) for o in ox]
    dy = [lax.rem(y - o + NY, NY) for o in oy]
    for s in range(STEPS):
        flags = (
            flag(owner_core[s] == core),
            flag(dx[s] == 0) * flag(dy[s] == 0),
            within(dx[s], 1, NX - 2), within(dy[s], 1, NY - 2),
            within(dx[s], 2, NX - 1), within(dy[s], 2, NY - 1),
            flag(oz[s] == z),
            flag(oa[s] > 0),
        )
        for n, f in enumerate(flags):
            masks[s, n] = jnp.full((rows_b, LANE), f.astype(jnp.float32)).astype(jnp.bfloat16)
    here = [(s, 0) for s in range(STEPS)]
    root = [(s, 1) for s in range(STEPS)]
    xplus = [(s, 2) for s in range(STEPS)]
    yplus = [(s, 3) for s in range(STEPS)]
    xminus = [(s, 4) for s in range(STEPS)]
    yminus = [(s, 5) for s in range(STEPS)]
    zroot = [(s, 6) for s in range(STEPS)]

    def pick(where, one, two):
        return jnp.where(masks[where[0], where[1]] > 0, one, two)

    def own_b(s, k, base, q):
        rows = pl.ds(pl.multiple_of(base + q * rows_b, rows_b), rows_b)
        return pick(here[s], bo_v[k, rows, :], bp_v[k, rows, :])

    def own_a(s, k):
        f = k // (256 // rows_b)
        rb = lax.rem(k, 256 // rows_b)
        rows = pl.ds(pl.multiple_of(rb * rows_b, rows_b), rows_b)
        low = a_v[rows, pl.ds(pl.multiple_of(f * LANE, LANE), LANE)]
        high = a_v[rows, pl.ds(pl.multiple_of(PANEL + f * LANE, LANE), LANE)]
        return pick((s, 7), high, low)

    def message(t, link):
        return pltpu.make_async_remote_copy(
            src_ref=sbuf.at[t, link], dst_ref=recv.at[t, link],
            send_sem=send_sem.at[t], recv_sem=recv_sem.at[t],
            device_id=links[link], device_id_type=MESH)

    def forward(t):
        return pltpu.make_async_remote_copy(
            src_ref=recv.at[t, pl.ds(0, 4)], dst_ref=precv.at[t],
            send_sem=f_send.at[t], recv_sem=f_recv.at[t],
            device_id=partner, device_id_type=MESH)

    def wait_all(ref, sem):
        pltpu.make_async_copy(ref, ref, sem).wait()

    def stage(t, relay):
        kb = jnp.minimum(t, nblk - 1)
        ka = jnp.minimum(t, ncol - 1)
        for s in range(STEPS):
            rows = pl.ds(s * rows_b, rows_b)
            for link, q, keep in ((0, 0, xplus), (2, 2, yplus), (1, 1, xminus), (3, 3, yminus)):
                value = own_b(s, kb, mine, q)
                if relay:
                    mate = {0: 2, 2: 0, 1: 3, 3: 1}[link]
                    moved = pick(keep[s], recv[t - DELAY, link, rows, :], recv[t - DELAY, mate, rows, :])
                    value = pick(root[s], value, moved)
                sbuf[t, link, rows, :] = value
            for link in (4, 5):
                value = own_a(s, ka)
                if relay:
                    value = pick(zroot[s], value, recv[t - DELAY, link, rows, :])
                sbuf[t, link, rows, :] = value
        for link in range(6):
            message(t, link).start()

    for t in range(DELAY):
        own_load(0, t).wait()
        partner_copy(0, t).wait_recv()
        stage(t, False)

    def step(t, carry):
        wait_all(recv.at[t - DELAY], recv_sem.at[t - DELAY])
        forward(t - DELAY).start()

        @pl.when(t < nblk)
        def _():
            own_load(0, t).wait()
            partner_copy(0, t).wait_recv()

        stage(t, True)
        return carry

    lax.fori_loop(DELAY, total, step, 0)

    def last(t, carry):
        wait_all(recv.at[t], recv_sem.at[t])
        forward(t).start()
        return carry

    lax.fori_loop(total - DELAY, total, last, 0)

    for s in range(STEPS):
        hz = lax.rem(z - oz[s] + nz, nz)
        up = flag(hz <= nz // 2)
        hop = choose(up, hz, nz - hz)
        link = 5 - up
        first = (hop - 1 + flag(hop == 0)) * DELAY

        def take_a(k, carry, s=s, link=link, first=first):
            got = recv[k + first, link, pl.ds(s * rows_b, rows_b), :]
            value = pick(zroot[s], own_a(s, k), got)
            f = k // (256 // rows_b)
            rb = lax.rem(k, 256 // rows_b)
            afull[pl.ds(pl.multiple_of(rb * rows_b, rows_b), rows_b),
                  pl.ds(pl.multiple_of(s * PANEL + f * LANE, LANE), LANE)] = value
            return carry

        lax.fori_loop(0, ncol, take_a, 0)

    load_c.wait()
    load_s.wait()
    for k in range(nblk):
        own_load(1, k).wait()
        partner_copy(1, k).wait_recv()

    def settle(t, carry):
        f = forward(t)
        f.wait_recv()
        return carry

    lax.fori_loop(0, total, settle, 0)

    def where_from(s):
        out = []
        for sign, i, j in ((0, dx[s], dy[s]),
                           (1, lax.rem(NX - dx[s], NX), lax.rem(NY - dy[s], NY))):
            i0 = flag(i == 0)
            j0 = flag(j == 0)
            hx = i + j + NX * i0 * (1 - j0)
            hy = i + j + NY * j0 * (1 - i0)
            near = i0 + j0 - i0 * j0
            tx = (hx - 1 + i0 * j0) * DELAY
            ty = (hy - 1 + i0 * j0) * DELAY
            out.append((sign, choose(near, sign, 2 + sign), choose(near, tx, ty)))
            out.append((2 + sign, choose(near, 2 + sign, sign), choose(near, ty, tx)))
        return out

    routes = [where_from(s) for s in range(STEPS)]

    def take_b(k, carry):
        for s in range(STEPS):
            for q, link, first in routes[s]:
                for src, base in ((recv, mine), (precv, other)):
                    got = src[k + first, link, pl.ds(s * rows_b, rows_b), :]
                    value = pick(root[s], own_b(s, k, base, q), got)
                    bfull[pl.ds(pl.multiple_of(s * PANEL + base + q * rows_b, rows_b), rows_b),
                          pl.ds(pl.multiple_of(k * LANE, LANE), LANE)] = value
        return carry

    lax.fori_loop(0, nblk, take_b, 0)

    width = nblk * LANE
    sk = jnp.zeros((256, LANE), jnp.float32)
    bs[...] = jnp.zeros_like(bs)
    at = 0
    while at < width:
        w = min(256, width - at)
        cols = pl.ds(at, w)
        b_c = bfull[:, cols]
        acc = jnp.dot(afull[...], b_c, preferred_element_type=jnp.float32)
        c_new = (c_v[:, cols].astype(jnp.float32) + acc).astype(jnp.bfloat16)
        cov[:, cols] = c_new
        s_c = s_v[cols, :]
        sk = sk + jnp.dot(c_new, s_c, preferred_element_type=jnp.float32)
        bs[...] += jnp.dot(b_c, s_c, preferred_element_type=jnp.float32)
        at += w
    put_c = pltpu.make_async_copy(cov, cout_hbm, out_sem.at[0])
    put_c.start()
    part[0] = sk
    pr = jnp.zeros((256, LANE), jnp.float32)
    rest = bs[...]
    for _ in range(3):
        piece = rest.astype(jnp.bfloat16)
        pr = pr + jnp.dot(afull[...], piece, preferred_element_type=jnp.float32)
        rest = rest - piece.astype(jnp.float32)
    part[1] = pr

    nr = 256 // nz

    def rows_of(j):
        return pl.ds(pl.multiple_of(j * nr, nr), nr)

    order = sorted(range(1, nz), key=lambda d: -min(d, nz - d))

    def scatter(d):
        to = lax.rem(z + d, nz)
        return pltpu.make_async_remote_copy(
            src_ref=part.at[:, rows_of(to), :], dst_ref=rsr.at[d - 1],
            send_sem=rs_sem.at[0], recv_sem=rs_sem.at[1],
            device_id=(r, to), device_id_type=MESH)

    def gather(d):
        to = lax.rem(z + d, nz)
        return pltpu.make_async_remote_copy(
            src_ref=red, dst_ref=outb.at[:, rows_of(z), :],
            send_sem=rs_sem.at[2], recv_sem=rs_sem.at[3],
            device_id=(r, to), device_id_type=MESH)

    for d in order:
        scatter(d).start()
    wait_all(rsr, rs_sem.at[1])
    value = part[:, rows_of(z), :]
    for d in range(nz - 1):
        value = value + rsr[d]
    red[...] = value
    outb[:, rows_of(z), :] = value
    for d in order:
        gather(d).start()
    wait_all(rsr, rs_sem.at[3])
    put_s = pltpu.make_async_copy(outb.at[0], sk_hbm, out_sem.at[1])
    put_p = pltpu.make_async_copy(outb.at[1], pr_hbm, out_sem.at[2])
    put_s.start()
    put_p.start()

    wait_all(rsr, rs_sem.at[0])
    wait_all(rsr, rs_sem.at[2])

    def drain(t, carry):
        wait_all(sbuf.at[t], send_sem.at[t])
        forward(t).wait_send()
        return carry

    lax.fori_loop(0, total, drain, 0)
    for k in range(nblk):
        for j in range(2):
            partner_copy(j, k).wait_send()
    put_c.wait()
    put_s.wait()
    put_p.wait()


def per_device(nz, a_tile, b_tile, c_prior, sketch_matrix, panel_ids):
    rows_b = 64
    seg = 2 * rows_b
    width = b_tile.shape[1]
    nblk = width // LANE
    rows_k = a_tile.shape[1]
    ncol = (PANEL // LANE) * (256 // rows_b)
    total = max(nblk + 6 * DELAY, ncol + (nz // 2 - 1) * DELAY)
    bf = jnp.bfloat16
    f32 = jnp.float32
    dma = pltpu.SemaphoreType.DMA
    dims = (nz, ncol, nblk, total, rows_b, rows_k)
    hbm = pl.BlockSpec(memory_space=pl.ANY)
    return pl.pallas_call(
        functools.partial(kernel, dims),
        out_shape=(
            jax.ShapeDtypeStruct((256, width), bf),
            jax.ShapeDtypeStruct((256, LANE), f32),
            jax.ShapeDtypeStruct((256, LANE), f32),
        ),
        in_specs=[pl.BlockSpec(memory_space=pltpu.SMEM)] + [hbm] * 4,
        out_specs=(hbm,) * 3,
        scratch_shapes=[
            pltpu.VMEM((256, rows_k), bf),
            pltpu.VMEM((nblk, PANEL, LANE), bf),
            pltpu.VMEM((nblk, PANEL, LANE), bf),
            pltpu.VMEM((256, width), bf),
            pltpu.VMEM((width, LANE), bf),
            pltpu.VMEM((total, 6, seg, LANE), bf),
            pltpu.VMEM((total, 6, seg, LANE), bf),
            pltpu.VMEM((total, 4, seg, LANE), bf),
            pltpu.VMEM((256, STEPS * PANEL), bf),
            pltpu.VMEM((STEPS * PANEL, width), bf),
            pltpu.VMEM((256, width), bf),
            pltpu.VMEM((2, 256, LANE), f32),
            pltpu.VMEM((nz - 1, 2, 256 // nz, LANE), f32),
            pltpu.VMEM((2, 256 // nz, LANE), f32),
            pltpu.VMEM((2, 256, LANE), f32),
            pltpu.VMEM((STEPS * PANEL, LANE), f32),
            pltpu.VMEM((STEPS, 8, rows_b, LANE), bf),
            dma((2, nblk)), dma((2, nblk)), dma((2, nblk)), dma((3,)),
            dma((total,)), dma((total,)), dma((total,)), dma((total,)),
            dma((4,)), dma((3,)),
        ],
        compiler_params=pltpu.CompilerParams(
            collective_id=0, has_side_effects=True, vmem_limit_bytes=60 * 1024 * 1024),
    )(panel_ids, a_tile, b_tile, c_prior, sketch_matrix)


def solution(mesh):
    placed = (P("row", "col"), P("row", "col"), P("row", "col"), P("col", None), P())
    return jax.shard_map(
        functools.partial(per_device, mesh.shape["col"]),
        mesh=mesh,
        in_specs=placed,
        out_specs=(P("row", "col"), P("row", None), P("row", None)),
        check_vma=False,
    )
```

```python
import functools

import jax
import jax.numpy as jnp
from jax import lax
from jax.experimental import pallas as pl
from jax.experimental.pallas import tpu as pltpu
from jax.sharding import PartitionSpec as P

PANEL = 512
STEPS = 2
NX = 4
NY = 4
LANE = 128
PART = 128
DELAY_A = 4
DELAY_B = 5
PIECES = ((0, 2), (2, 6), (6, 13))
MESH = pl.DeviceIdType.MESH


def kernel(dims, ids, a_hbm, b_hbm, c_hbm, s_hbm, cout_hbm, sk_hbm, pr_hbm,
           ab_v, bo_v, bp_v, c_v, s_v, sb, sa, rb, ra, afull, bfull, cov,
           part, rsr, red, outb, bs, masks,
           in_sem, bo_sem, bp_send, bp_recv, ap_sem,
           sb_sem, rb_sem, sa_sem, ra_sem, fb_send, fb_recv, fa_send, fa_recv,
           rs_sem, out_sem):
    nz, na, nb, ta, tb, rows_k = dims
    r = lax.axis_index("row")
    z = lax.axis_index("col")
    core = lax.rem(r, 2)
    chip = r // 2
    x = lax.rem(chip, NX)
    y = chip // NX
    first_core = core == 0
    second_core = core == 1

    def at_chip(yy, xx):
        return (lax.rem(yy + NY, NY) * NX + lax.rem(xx + NX, NX)) * 2 + core

    partner = (chip * 2 + (1 - core), z)
    plane = ((at_chip(y, x + 1), z), (at_chip(y, x - 1), z),
             (at_chip(y + 1, x), z), (at_chip(y - 1, x), z))
    line = ((r, lax.rem(z + 1, nz)), (r, lax.rem(z + nz - 1, nz)))

    def piece(j):
        low, high = PIECES[j]
        return pl.ds(low * LANE, (high - low) * LANE)

    def own_load(j):
        return pltpu.make_async_copy(b_hbm.at[:, piece(j)], bo_v.at[:, piece(j)], bo_sem.at[j])

    def partner_copy(j):
        return pltpu.make_async_remote_copy(
            src_ref=bo_v.at[:, piece(j)], dst_ref=bp_v.at[:, piece(j)],
            send_sem=bp_send.at[j], recv_sem=bp_recv.at[j],
            device_id=partner, device_id_type=MESH)

    load_a = pltpu.make_async_copy(a_hbm, ab_v.at[core], in_sem.at[0])
    load_c = pltpu.make_async_copy(c_hbm, c_v, in_sem.at[1])
    load_s = pltpu.make_async_copy(s_hbm, s_v, in_sem.at[2])
    partner_a = pltpu.make_async_remote_copy(
        src_ref=ab_v.at[0], dst_ref=ab_v.at[0], send_sem=ap_sem.at[0], recv_sem=ap_sem.at[1],
        device_id=partner, device_id_type=MESH)
    npc = len(PIECES)

    barrier = pltpu.get_barrier_semaphore()
    pl.semaphore_signal(barrier, inc=1, device_id=partner, device_id_type=MESH)

    @pl.when(first_core)
    def _():
        for target in plane:
            pl.semaphore_signal(barrier, inc=1, device_id=target, device_id_type=MESH)

    @pl.when(second_core)
    def _():
        for target in line:
            pl.semaphore_signal(barrier, inc=1, device_id=target, device_id_type=MESH)

    load_a.start()
    for j in range(npc):
        own_load(j).start()

    def flag(cond):
        return cond.astype(jnp.int32)

    def choose(cond, one, two):
        return two + cond * (one - two)

    def within(v, low, high):
        return flag(v >= low) * flag(v <= high)

    pid = [ids[s] for s in range(STEPS)]
    owner_core = [lax.rem(p, 2) for p in pid]
    ox = [lax.rem(lax.div(p, 2), NX) for p in pid]
    oy = [lax.div(p, 2 * NX) for p in pid]
    oz = [lax.div(p * PANEL, rows_k) for p in pid]
    oa = [lax.rem(p * PANEL, rows_k) for p in pid]
    dx = [[lax.rem(g * (x - o) + NX, NX) for o in ox] for g in (1, -1)]
    dy = [[lax.rem(g * (y - o) + NY, NY) for o in oy] for g in (1, -1)]
    for s in range(STEPS):
        flags = (
            flag(owner_core[s] == core), flag(dx[0][s] == 0) * flag(dy[0][s] == 0),
            within(dx[0][s], 1, NX - 2), within(dx[1][s], 1, NX - 2),
            within(dy[0][s], 1, NY - 2), within(dy[1][s], 1, NY - 2),
            flag(oz[s] == z), flag(oa[s] > 0),
        )
        for n, f in enumerate(flags):
            masks[s, n] = jnp.full((PART, LANE), f.astype(jnp.float32)).astype(jnp.bfloat16)
    HERE, ROOT, KEEP, ZROOT, HIGH = 0, 1, 2, 6, 7

    def pick(s, n, one, two):
        return jnp.where(masks[s, n] > 0, one, two)

    def lanes(k):
        return pl.ds(pl.multiple_of(k * LANE, LANE), LANE)

    def own_b(s, k, base):
        rows = pl.ds(pl.multiple_of(base, PART), PART)
        return pick(s, HERE, bo_v[rows, lanes(k)], bp_v[rows, lanes(k)])

    def own_a(s, f, tile, j):
        rows = pl.ds(pl.multiple_of(j * PART, PART), PART)
        return pick(s, HIGH, ab_v[tile, rows, lanes(PANEL // LANE + f)], ab_v[tile, rows, lanes(f)])

    def send_b(t, link):
        return pltpu.make_async_remote_copy(
            src_ref=sb.at[t, link], dst_ref=rb.at[t, link],
            send_sem=sb_sem.at[t], recv_sem=rb_sem.at[t],
            device_id=plane[link], device_id_type=MESH)

    def send_a(t, link, src):
        return pltpu.make_async_remote_copy(
            src_ref=src, dst_ref=ra.at[t, link],
            send_sem=sa_sem.at[t], recv_sem=ra_sem.at[t],
            device_id=line[link], device_id_type=MESH)

    def share_b(t):
        return pltpu.make_async_remote_copy(
            src_ref=rb.at[t], dst_ref=rb.at[t],
            send_sem=fb_send.at[t], recv_sem=fb_recv.at[t],
            device_id=partner, device_id_type=MESH)

    def share_a(t):
        return pltpu.make_async_remote_copy(
            src_ref=ra.at[t], dst_ref=ra.at[t],
            send_sem=fa_send.at[t], recv_sem=fa_recv.at[t],
            device_id=partner, device_id_type=MESH)

    def wait_all(ref, sem):
        pltpu.make_async_copy(ref, ref, sem).wait()

    def stage_b(t, own, relay):
        for link, sign in ((0, 0), (1, 1), (2, 0), (3, 1)):
            mate = (link + 2) % 4
            q = link // 2
            for s in range(STEPS):
                rows = pl.ds(s * PART, PART)
                value = None
                if relay:
                    value = pick(s, KEEP + link, rb[t - DELAY_B, link, rows, :],
                                 rb[t - DELAY_B, mate, rows, :])
                if own:
                    mine = own_b(s, t, sign * (PANEL // 2) + q * PART)
                    value = pick(s, ROOT, mine, value) if relay else mine
                sb[t, link, rows, :] = value
            send_b(t, link).start()

    def stage_a(t, relay):
        for s in range(STEPS):
            rows = pl.ds(s * PART, PART)
            value = own_a(s, t // 4, lax.rem(t, 4) // 2, lax.rem(t, 2))
            for link in range(2):
                sa[t, link, rows, :] = (
                    pick(s, ZROOT, value, ra[t - DELAY_A, link, rows, :]) if relay else value)
        for link in range(2):
            send_a(t, link, sa.at[t, link]).start()

    @pl.when(first_core)
    def _():
        load_a.wait()
        pl.semaphore_wait(barrier, 5)
        partner_a.start()
        for t in range(DELAY_B):
            for j, (low, _) in enumerate(PIECES):
                if low == t:
                    own_load(j).wait()
                    partner_copy(j).start()
                    partner_copy(j).wait_recv()
            stage_b(t, True, False)
        load_c.start()
        load_s.start()

        def begin(t, carry):
            for j, (low, _) in enumerate(PIECES):
                if low >= DELAY_B:
                    @pl.when(t == low)
                    def _(j=j):
                        own_load(j).wait()
                        partner_copy(j).start()
                        partner_copy(j).wait_recv()

            wait_all(rb.at[t - DELAY_B], rb_sem.at[t - DELAY_B])
            stage_b(t, True, True)
            share_b(t - DELAY_B).start()
            return carry

        def relay(t, carry):
            wait_all(rb.at[t - DELAY_B], rb_sem.at[t - DELAY_B])
            stage_b(t, False, True)
            share_b(t - DELAY_B).start()
            return carry

        def last(t, carry):
            wait_all(rb.at[t], rb_sem.at[t])
            share_b(t).start()
            return carry

        lax.fori_loop(DELAY_B, nb, begin, 0)
        lax.fori_loop(nb, tb, relay, 0)
        lax.fori_loop(tb - DELAY_B, tb, last, 0)

    @pl.when(second_core)
    def _():
        pl.semaphore_wait(barrier, 3)
        for j in range(npc):
            own_load(j).wait()
            partner_copy(j).start()
        load_a.wait()
        partner_a.wait_recv()
        for t in range(DELAY_A):
            stage_a(t, False)
        load_c.start()
        load_s.start()

        def begin(t, carry):
            wait_all(ra.at[t - DELAY_A], ra_sem.at[t - DELAY_A])
            stage_a(t, True)
            share_a(t - DELAY_A).start()
            return carry

        def relay(t, carry):
            wait_all(ra.at[t - DELAY_A], ra_sem.at[t - DELAY_A])
            for link in range(2):
                send_a(t, link, ra.at[t - DELAY_A, link]).start()
            share_a(t - DELAY_A).start()
            return carry

        def last(t, carry):
            wait_all(ra.at[t], ra_sem.at[t])
            share_a(t).start()
            return carry

        lax.fori_loop(DELAY_A, na, begin, 0)
        lax.fori_loop(na, ta, relay, 0)
        lax.fori_loop(ta - DELAY_A, ta, last, 0)
        for j in range(npc):
            partner_copy(j).wait_recv()

        def settle(t, carry):
            wait_all(rb.at[t], fb_recv.at[t])
            return carry

        lax.fori_loop(0, tb, settle, 0)

    load_c.wait()
    load_s.wait()

    routes = []
    for s in range(STEPS):
        for g in range(2):
            i, j = dx[g][s], dy[g][s]
            i0, j0 = flag(i == 0), flag(j == 0)
            near = i0 + j0 - i0 * j0
            tx = (i + j + NX * i0 * (1 - j0) - 1 + i0 * j0) * DELAY_B
            ty = (i + j + NY * j0 * (1 - i0) - 1 + i0 * j0) * DELAY_B
            routes.append((s, g, 0, g + 2 * (1 - near), choose(near, tx, ty)))
            routes.append((s, g, 1, g + 2 * near, choose(near, ty, tx)))

    def take_b(k, carry):
        for s, g, q, link, first in routes:
            base = g * (PANEL // 2) + q * PART
            got = rb[k + first, link, pl.ds(s * PART, PART), :]
            bfull[pl.ds(s * PANEL + base, PART), lanes(k)] = pick(s, ROOT, own_b(s, k, base), got)
        return carry

    lax.fori_loop(0, nb, take_b, 0)

    width = nb * LANE
    blocks = [pl.ds(at, min(256, width - at)) for at in range(0, width, 256)]
    bs[...] = jnp.zeros_like(bs)
    for cols in blocks:
        bs[...] += jnp.dot(bfull[:, cols], s_v[cols, :], preferred_element_type=jnp.float32)

    @pl.when(first_core)
    def _():
        def settle(t, carry):
            wait_all(ra.at[t], fa_recv.at[t])
            return carry

        lax.fori_loop(0, ta, settle, 0)

    for s in range(STEPS):
        hz = lax.rem(z - oz[s] + nz, nz)
        down = flag(hz > nz // 2)
        hop = choose(down, nz - hz, hz)
        first = (hop - 1 + flag(hop == 0)) * DELAY_A
        for f in range(PANEL // LANE):
            for j in range(2):
                got = ra[first + 4 * f + 2 * core + j, down, pl.ds(s * PART, PART), :]
                afull[pl.ds(j * PART, PART), pl.ds(s * PANEL + f * LANE, LANE)] = pick(
                    s, ZROOT, own_a(s, f, core, j), got)

    nr = 256 // nz

    def rows_of(j):
        return pl.ds(pl.multiple_of(j * nr, nr), nr)

    order = sorted(range(1, nz), key=lambda d: -min(d, nz - d))

    def scatter(n, d):
        to = lax.rem(z + d, nz)
        return pltpu.make_async_remote_copy(
            src_ref=part.at[n, rows_of(to), :], dst_ref=rsr.at[n, d - 1],
            send_sem=rs_sem.at[n, 0], recv_sem=rs_sem.at[n, 1],
            device_id=(r, to), device_id_type=MESH)

    def gather(n, d):
        to = lax.rem(z + d, nz)
        return pltpu.make_async_remote_copy(
            src_ref=red.at[n], dst_ref=outb.at[n, rows_of(z), :],
            send_sem=rs_sem.at[n, 2], recv_sem=rs_sem.at[n, 3],
            device_id=(r, to), device_id_type=MESH)

    def reduce(n):
        wait_all(rsr.at[n], rs_sem.at[n, 1])
        value = part[n, rows_of(z), :]
        for d in range(nz - 1):
            value = value + rsr[n, d]
        red[n] = value
        outb[n, rows_of(z), :] = value
        for d in order:
            gather(n, d).start()

    pr = jnp.zeros((256, LANE), jnp.float32)
    rest = bs[...]
    for _ in range(3):
        term = rest.astype(jnp.bfloat16)
        pr = pr + jnp.dot(afull[...], term, preferred_element_type=jnp.float32)
        rest = rest - term.astype(jnp.float32)
    part[1] = pr
    for d in order:
        scatter(1, d).start()
    sk = jnp.zeros((256, LANE), jnp.float32)
    for cols in blocks:
        acc = jnp.dot(afull[...], bfull[:, cols], preferred_element_type=jnp.float32)
        c_new = (c_v[:, cols].astype(jnp.float32) + acc).astype(jnp.bfloat16)
        cov[:, cols] = c_new
        sk = sk + jnp.dot(c_new, s_v[cols, :], preferred_element_type=jnp.float32)
    part[0] = sk
    for d in order:
        scatter(0, d).start()
    put_c = pltpu.make_async_copy(cov, cout_hbm, out_sem.at[0])
    put_c.start()
    reduce(1)
    reduce(0)

    @pl.when(first_core)
    def _():
        def drain(t, carry):
            wait_all(sb.at[t], sb_sem.at[t])
            share_b(t).wait_send()
            return carry

        lax.fori_loop(0, tb, drain, 0)
        partner_a.wait_send()

    @pl.when(second_core)
    def _():
        def drain(t, carry):
            wait_all(sa.at[0], sa_sem.at[t])
            share_a(t).wait_send()
            return carry

        lax.fori_loop(0, ta, drain, 0)

    for j in range(npc):
        partner_copy(j).wait_send()
    wait_all(rsr.at[1], rs_sem.at[1, 0])
    wait_all(rsr.at[0], rs_sem.at[0, 0])
    wait_all(rsr.at[1], rs_sem.at[1, 2])
    put_c.wait()
    wait_all(rsr.at[1], rs_sem.at[1, 3])
    put_p = pltpu.make_async_copy(outb.at[1], pr_hbm, out_sem.at[2])
    put_p.start()
    wait_all(rsr.at[0], rs_sem.at[0, 3])
    put_s = pltpu.make_async_copy(outb.at[0], sk_hbm, out_sem.at[1])
    put_s.start()
    wait_all(rsr.at[0], rs_sem.at[0, 2])
    put_s.wait()
    put_p.wait()


def per_device(nz, a_tile, b_tile, c_prior, sketch_matrix, panel_ids):
    width = b_tile.shape[1]
    nb = width // LANE
    rows_k = a_tile.shape[1]
    na = (PANEL // LANE) * (2 * 256 // PART)
    tb = nb + 6 * DELAY_B
    ta = na + (nz // 2 - 1) * DELAY_A
    bf = jnp.bfloat16
    f32 = jnp.float32
    dma = pltpu.SemaphoreType.DMA
    vmem = pltpu.VMEM
    nr = 256 // nz
    npc = len(PIECES)
    hbm = pl.BlockSpec(memory_space=pl.ANY)
    return pl.pallas_call(
        functools.partial(kernel, (nz, na, nb, ta, tb, rows_k)),
        out_shape=(
            jax.ShapeDtypeStruct((256, width), bf),
            jax.ShapeDtypeStruct((256, LANE), f32),
            jax.ShapeDtypeStruct((256, LANE), f32),
        ),
        in_specs=[pl.BlockSpec(memory_space=pltpu.SMEM)] + [hbm] * 4,
        out_specs=(hbm,) * 3,
        scratch_shapes=[
            vmem((2, 256, rows_k), bf),
            vmem((PANEL, width), bf),
            vmem((PANEL, width), bf),
            vmem((256, width), bf),
            vmem((width, LANE), bf),
            vmem((tb, 4, STEPS * PART, LANE), bf),
            vmem((na, 2, STEPS * PART, LANE), bf),
            vmem((tb, 4, STEPS * PART, LANE), bf),
            vmem((ta, 2, STEPS * PART, LANE), bf),
            vmem((256, STEPS * PANEL), bf),
            vmem((STEPS * PANEL, width), bf),
            vmem((256, width), bf),
            vmem((2, 256, LANE), f32),
            vmem((2, nz - 1, nr, LANE), f32),
            vmem((2, nr, LANE), f32),
            vmem((2, 256, LANE), f32),
            vmem((STEPS * PANEL, LANE), f32),
            vmem((STEPS, 8, PART, LANE), bf),
            dma((3,)), dma((npc,)), dma((npc,)), dma((npc,)), dma((2,)),
            dma((tb,)), dma((tb,)), dma((ta,)), dma((ta,)),
            dma((tb,)), dma((tb,)), dma((ta,)), dma((ta,)),
            dma((2, 4)), dma((3,)),
        ],
        compiler_params=pltpu.CompilerParams(
            collective_id=0, has_side_effects=True, vmem_limit_bytes=60 * 1024 * 1024),
    )(panel_ids, a_tile, b_tile, c_prior, sketch_matrix)


def solution(mesh):
    placed = (P("row", "col"), P("row", "col"), P("row", "col"), P("col", None), P())
    return jax.shard_map(
        functools.partial(per_device, mesh.shape["col"]),
        mesh=mesh,
        in_specs=placed,
        out_specs=(P("row", "col"), P("row", None), P("row", None)),
        check_vma=False,
    )
```

```python
import functools

import jax
import jax.numpy as jnp
from jax import lax
from jax.experimental import pallas as pl
from jax.experimental.pallas import tpu as pltpu
from jax.sharding import PartitionSpec as P

PANEL = 512
STEPS = 2
NX = 4
NY = 4
LANE = 128
PART = 128
TILE = 16
DELAY_A = 4
DELAY_B = 5
PIECES = ((0, 2), (2, 6), (6, 13))
MESH = pl.DeviceIdType.MESH


def kernel(dims, ids, a_hbm, b_hbm, c_hbm, s_hbm, cout_hbm, sk_hbm, pr_hbm,
           ab_v, bo_v, bp_v, c_v, s_v, sb, sa, rb, ra, afull, bfull, cov,
           part, rsr, red, outg, outb, bs, masks,
           in_sem, bo_sem, bp_send, bp_recv, ap_sem,
           sb_sem, rb_sem, sa_sem, ra_sem, fb_send, fb_recv, fa_send, fa_recv,
           rs_sem, out_sem):
    nz, na, nb, ta, tb, rows_k = dims
    r = lax.axis_index("row")
    z = lax.axis_index("col")
    core = lax.rem(r, 2)
    chip = r // 2
    x = lax.rem(chip, NX)
    y = chip // NX
    first_core = core == 0
    second_core = core == 1

    def at_chip(yy, xx):
        return (lax.rem(yy + NY, NY) * NX + lax.rem(xx + NX, NX)) * 2 + core

    partner = (chip * 2 + (1 - core), z)
    plane = ((at_chip(y, x + 1), z), (at_chip(y, x - 1), z),
             (at_chip(y + 1, x), z), (at_chip(y - 1, x), z))
    line = ((r, lax.rem(z + 1, nz)), (r, lax.rem(z + nz - 1, nz)))

    def piece(j):
        low, high = PIECES[j]
        return pl.ds(low * LANE, (high - low) * LANE)

    def own_load(j):
        return pltpu.make_async_copy(b_hbm.at[:, piece(j)], bo_v.at[:, piece(j)], bo_sem.at[j])

    def partner_copy(j):
        return pltpu.make_async_remote_copy(
            src_ref=bo_v.at[:, piece(j)], dst_ref=bp_v.at[:, piece(j)],
            send_sem=bp_send.at[j], recv_sem=bp_recv.at[j],
            device_id=partner, device_id_type=MESH)

    load_a = pltpu.make_async_copy(a_hbm, ab_v.at[core], in_sem.at[0])
    load_c = pltpu.make_async_copy(c_hbm, c_v, in_sem.at[1])
    load_s = pltpu.make_async_copy(s_hbm, s_v, in_sem.at[2])
    partner_a = pltpu.make_async_remote_copy(
        src_ref=ab_v.at[0], dst_ref=ab_v.at[0], send_sem=ap_sem.at[0], recv_sem=ap_sem.at[1],
        device_id=partner, device_id_type=MESH)
    npc = len(PIECES)

    barrier = pltpu.get_barrier_semaphore()
    pl.semaphore_signal(barrier, inc=1, device_id=partner, device_id_type=MESH)

    @pl.when(first_core)
    def _():
        for target in plane:
            pl.semaphore_signal(barrier, inc=1, device_id=target, device_id_type=MESH)

    @pl.when(second_core)
    def _():
        for target in line:
            pl.semaphore_signal(barrier, inc=1, device_id=target, device_id_type=MESH)

    load_a.start()
    for j in range(npc):
        own_load(j).start()

    def flag(cond):
        return cond.astype(jnp.int32)

    def choose(cond, one, two):
        return two + cond * (one - two)

    def within(v, low, high):
        return flag(v >= low) * flag(v <= high)

    pid = [ids[s] for s in range(STEPS)]
    owner_core = [lax.rem(p, 2) for p in pid]
    ox = [lax.rem(lax.div(p, 2), NX) for p in pid]
    oy = [lax.div(p, 2 * NX) for p in pid]
    oz = [lax.div(p * PANEL, rows_k) for p in pid]
    oa = [lax.rem(p * PANEL, rows_k) for p in pid]
    dx = [[lax.rem(g * (x - o) + NX, NX) for o in ox] for g in (1, -1)]
    dy = [[lax.rem(g * (y - o) + NY, NY) for o in oy] for g in (1, -1)]
    for s in range(STEPS):
        flags = (
            flag(owner_core[s] == core), flag(dx[0][s] == 0) * flag(dy[0][s] == 0),
            within(dx[0][s], 1, NX - 2), within(dx[1][s], 1, NX - 2),
            within(dy[0][s], 1, NY - 2), within(dy[1][s], 1, NY - 2),
            flag(oz[s] == z), flag(oa[s] > 0),
        )
        for n, f in enumerate(flags):
            masks[s, n] = jnp.full((TILE, LANE), f.astype(jnp.float32)).astype(jnp.bfloat16)
    HERE, ROOT, KEEP, ZROOT, HIGH = 0, 1, 2, 6, 7

    def pick(s, n, one, two):
        keep = jnp.concatenate([masks[s, n]] * (PART // TILE), axis=0) > 0
        return jnp.where(keep, one, two)

    def lanes(k):
        return pl.ds(pl.multiple_of(k * LANE, LANE), LANE)

    def own_b(s, k, base):
        rows = pl.ds(pl.multiple_of(base, PART), PART)
        return pick(s, HERE, bo_v[rows, lanes(k)], bp_v[rows, lanes(k)])

    def own_a(s, f, tile, j):
        rows = pl.ds(pl.multiple_of(j * PART, PART), PART)
        return pick(s, HIGH, ab_v[tile, rows, lanes(PANEL // LANE + f)], ab_v[tile, rows, lanes(f)])

    def send_b(t, link):
        return pltpu.make_async_remote_copy(
            src_ref=sb.at[t, link], dst_ref=rb.at[t, link],
            send_sem=sb_sem.at[t], recv_sem=rb_sem.at[t],
            device_id=plane[link], device_id_type=MESH)

    def send_a(t, link, src):
        return pltpu.make_async_remote_copy(
            src_ref=src, dst_ref=ra.at[t, link],
            send_sem=sa_sem.at[t], recv_sem=ra_sem.at[t],
            device_id=line[link], device_id_type=MESH)

    def share_b(t):
        return pltpu.make_async_remote_copy(
            src_ref=rb.at[t], dst_ref=rb.at[t],
            send_sem=fb_send.at[t], recv_sem=fb_recv.at[t],
            device_id=partner, device_id_type=MESH)

    def share_a(t):
        return pltpu.make_async_remote_copy(
            src_ref=ra.at[t], dst_ref=ra.at[t],
            send_sem=fa_send.at[t], recv_sem=fa_recv.at[t],
            device_id=partner, device_id_type=MESH)

    def wait_all(ref, sem):
        pltpu.make_async_copy(ref, ref, sem).wait()

    def stage_b(t, own, relay):
        for link, sign in ((0, 0), (1, 1), (2, 0), (3, 1)):
            mate = (link + 2) % 4
            q = link // 2
            for s in range(STEPS):
                rows = pl.ds(s * PART, PART)
                value = None
                if relay:
                    value = pick(s, KEEP + link, rb[t - DELAY_B, link, rows, :],
                                 rb[t - DELAY_B, mate, rows, :])
                if own:
                    mine = own_b(s, t, sign * (PANEL // 2) + q * PART)
                    value = pick(s, ROOT, mine, value) if relay else mine
                sb[t, link, rows, :] = value
            send_b(t, link).start()

    def stage_a(t, relay):
        for s in range(STEPS):
            rows = pl.ds(s * PART, PART)
            value = own_a(s, t // 4, lax.rem(t, 4) // 2, lax.rem(t, 2))
            for link in range(2):
                sa[t, link, rows, :] = (
                    pick(s, ZROOT, value, ra[t - DELAY_A, link, rows, :]) if relay else value)
        for link in range(2):
            send_a(t, link, sa.at[t, link]).start()

    @pl.when(first_core)
    def _():
        load_a.wait()
        pl.semaphore_wait(barrier, 5)
        partner_a.start()
        for t in range(DELAY_B):
            for j, (low, _) in enumerate(PIECES):
                if low == t:
                    own_load(j).wait()
                    partner_copy(j).start()
                    partner_copy(j).wait_recv()
            stage_b(t, True, False)
        load_c.start()
        load_s.start()

        def begin(t, carry):
            for j, (low, _) in enumerate(PIECES):
                if low >= DELAY_B:
                    @pl.when(t == low)
                    def _(j=j):
                        own_load(j).wait()
                        partner_copy(j).start()
                        partner_copy(j).wait_recv()

            wait_all(rb.at[t - DELAY_B], rb_sem.at[t - DELAY_B])
            stage_b(t, True, True)
            share_b(t - DELAY_B).start()
            return carry

        def relay(t, carry):
            wait_all(rb.at[t - DELAY_B], rb_sem.at[t - DELAY_B])
            stage_b(t, False, True)
            share_b(t - DELAY_B).start()
            return carry

        def last(t, carry):
            wait_all(rb.at[t], rb_sem.at[t])
            share_b(t).start()
            return carry

        lax.fori_loop(DELAY_B, nb, begin, 0)
        lax.fori_loop(nb, tb, relay, 0)
        lax.fori_loop(tb - DELAY_B, tb, last, 0)

    @pl.when(second_core)
    def _():
        pl.semaphore_wait(barrier, 3)
        for j in range(npc):
            own_load(j).wait()
            partner_copy(j).start()
        load_a.wait()
        partner_a.wait_recv()
        for t in range(DELAY_A):
            stage_a(t, False)
        load_c.start()
        load_s.start()

        def begin(t, carry):
            wait_all(ra.at[t - DELAY_A], ra_sem.at[t - DELAY_A])
            stage_a(t, True)
            share_a(t - DELAY_A).start()
            return carry

        def relay(t, carry):
            wait_all(ra.at[t - DELAY_A], ra_sem.at[t - DELAY_A])
            for link in range(2):
                send_a(t, link, ra.at[t - DELAY_A, link]).start()
            share_a(t - DELAY_A).start()
            return carry

        def last(t, carry):
            wait_all(ra.at[t], ra_sem.at[t])
            share_a(t).start()
            return carry

        lax.fori_loop(DELAY_A, na, begin, 0)
        lax.fori_loop(na, ta, relay, 0)
        lax.fori_loop(ta - DELAY_A, ta, last, 0)
        for j in range(npc):
            partner_copy(j).wait_recv()

        def settle(t, carry):
            wait_all(rb.at[t], fb_recv.at[t])
            return carry

        lax.fori_loop(0, tb, settle, 0)

    load_c.wait()
    load_s.wait()

    routes = []
    for s in range(STEPS):
        for g in range(2):
            i, j = dx[g][s], dy[g][s]
            i0, j0 = flag(i == 0), flag(j == 0)
            near = i0 + j0 - i0 * j0
            tx = (i + j + NX * i0 * (1 - j0) - 1 + i0 * j0) * DELAY_B
            ty = (i + j + NY * j0 * (1 - i0) - 1 + i0 * j0) * DELAY_B
            routes.append((s, g, 0, g + 2 * (1 - near), choose(near, tx, ty)))
            routes.append((s, g, 1, g + 2 * near, choose(near, ty, tx)))

    def take_b(k, carry):
        for s, g, q, link, first in routes:
            base = g * (PANEL // 2) + q * PART
            got = rb[k + first, link, pl.ds(s * PART, PART), :]
            bfull[pl.ds(s * PANEL + base, PART), lanes(k)] = pick(s, ROOT, own_b(s, k, base), got)
        return carry

    lax.fori_loop(0, nb, take_b, 0)

    width = nb * LANE
    blocks = [pl.ds(at, min(256, width - at)) for at in range(0, width, 256)]
    bs[...] = jnp.zeros_like(bs)
    for cols in blocks:
        bs[...] += jnp.dot(bfull[:, cols], s_v[cols, :], preferred_element_type=jnp.float32)

    @pl.when(first_core)
    def _():
        def settle(t, carry):
            wait_all(ra.at[t], fa_recv.at[t])
            return carry

        lax.fori_loop(0, ta, settle, 0)

    for s in range(STEPS):
        hz = lax.rem(z - oz[s] + nz, nz)
        down = flag(hz > nz // 2)
        hop = choose(down, nz - hz, hz)
        first = (hop - 1 + flag(hop == 0)) * DELAY_A
        for f in range(PANEL // LANE):
            for j in range(2):
                got = ra[first + 4 * f + 2 * core + j, down, pl.ds(s * PART, PART), :]
                afull[pl.ds(j * PART, PART), pl.ds(s * PANEL + f * LANE, LANE)] = pick(
                    s, ZROOT, own_a(s, f, core, j), got)

    nr = 256 // nz

    def rows_of(j):
        return pl.ds(pl.multiple_of(j * nr, nr), nr)

    order = sorted(range(1, nz), key=lambda d: -min(d, nz - d))

    def scatter(n, d):
        to = lax.rem(z + d, nz)
        return pltpu.make_async_remote_copy(
            src_ref=part.at[n, rows_of(to), :], dst_ref=rsr.at[n, d - 1],
            send_sem=rs_sem.at[n, 0], recv_sem=rs_sem.at[n, 1],
            device_id=(r, to), device_id_type=MESH)

    def gather(n, d):
        to = lax.rem(z + d, nz)
        return pltpu.make_async_remote_copy(
            src_ref=red.at[n], dst_ref=outg.at[n, rows_of(z), :],
            send_sem=rs_sem.at[n, 2], recv_sem=rs_sem.at[n, 3],
            device_id=(r, to), device_id_type=MESH)

    def reduce(n):
        wait_all(rsr.at[n], rs_sem.at[n, 1])
        value = part[n, rows_of(z), :]
        for d in range(nz - 1):
            value = value + rsr[n, d]
        red[n] = value.astype(jnp.bfloat16)
        outg[n, rows_of(z), :] = value.astype(jnp.bfloat16)
        for d in order:
            gather(n, d).start()

    pr = jnp.zeros((256, LANE), jnp.float32)
    rest = bs[...]
    for _ in range(3):
        term = rest.astype(jnp.bfloat16)
        pr = pr + jnp.dot(afull[...], term, preferred_element_type=jnp.float32)
        rest = rest - term.astype(jnp.float32)
    part[1] = pr
    for d in order:
        scatter(1, d).start()
    sk = jnp.zeros((256, LANE), jnp.float32)
    for cols in blocks:
        acc = jnp.dot(afull[...], bfull[:, cols], preferred_element_type=jnp.float32)
        c_new = (c_v[:, cols].astype(jnp.float32) + acc).astype(jnp.bfloat16)
        cov[:, cols] = c_new
        sk = sk + jnp.dot(c_new, s_v[cols, :], preferred_element_type=jnp.float32)
    part[0] = sk
    for d in order:
        scatter(0, d).start()
    put_c = pltpu.make_async_copy(cov, cout_hbm, out_sem.at[0])
    put_c.start()
    reduce(1)
    reduce(0)

    @pl.when(first_core)
    def _():
        def drain(t, carry):
            wait_all(sb.at[t], sb_sem.at[t])
            share_b(t).wait_send()
            return carry

        lax.fori_loop(0, tb, drain, 0)
        partner_a.wait_send()

    @pl.when(second_core)
    def _():
        def drain(t, carry):
            wait_all(sa.at[0], sa_sem.at[t])
            share_a(t).wait_send()
            return carry

        lax.fori_loop(0, ta, drain, 0)

    for j in range(npc):
        partner_copy(j).wait_send()
    wait_all(rsr.at[1], rs_sem.at[1, 0])
    wait_all(rsr.at[0], rs_sem.at[0, 0])
    others = pl.ds(0, 256 - nr)
    wait_all(outg.at[1, others], rs_sem.at[1, 2])
    put_c.wait()
    wait_all(outg.at[1, others], rs_sem.at[1, 3])
    outb[1] = outg[1].astype(jnp.float32)
    put_p = pltpu.make_async_copy(outb.at[1], pr_hbm, out_sem.at[2])
    put_p.start()
    wait_all(outg.at[0, others], rs_sem.at[0, 3])
    outb[0] = outg[0].astype(jnp.float32)
    put_s = pltpu.make_async_copy(outb.at[0], sk_hbm, out_sem.at[1])
    put_s.start()
    wait_all(outg.at[0, others], rs_sem.at[0, 2])
    put_s.wait()
    put_p.wait()


def per_device(nz, a_tile, b_tile, c_prior, sketch_matrix, panel_ids):
    width = b_tile.shape[1]
    nb = width // LANE
    rows_k = a_tile.shape[1]
    na = (PANEL // LANE) * (2 * 256 // PART)
    tb = nb + 6 * DELAY_B
    ta = na + (nz // 2 - 1) * DELAY_A
    bf = jnp.bfloat16
    f32 = jnp.float32
    dma = pltpu.SemaphoreType.DMA
    vmem = pltpu.VMEM
    nr = 256 // nz
    npc = len(PIECES)
    hbm = pl.BlockSpec(memory_space=pl.ANY)
    return pl.pallas_call(
        functools.partial(kernel, (nz, na, nb, ta, tb, rows_k)),
        out_shape=(
            jax.ShapeDtypeStruct((256, width), bf),
            jax.ShapeDtypeStruct((256, LANE), f32),
            jax.ShapeDtypeStruct((256, LANE), f32),
        ),
        in_specs=[pl.BlockSpec(memory_space=pltpu.SMEM)] + [hbm] * 4,
        out_specs=(hbm,) * 3,
        scratch_shapes=[
            vmem((2, 256, rows_k), bf),
            vmem((PANEL, width), bf),
            vmem((PANEL, width), bf),
            vmem((256, width), bf),
            vmem((width, LANE), bf),
            vmem((tb, 4, STEPS * PART, LANE), bf),
            vmem((na, 2, STEPS * PART, LANE), bf),
            vmem((tb, 4, STEPS * PART, LANE), bf),
            vmem((ta, 2, STEPS * PART, LANE), bf),
            vmem((256, STEPS * PANEL), bf),
            vmem((STEPS * PANEL, width), bf),
            vmem((256, width), bf),
            vmem((2, 256, LANE), f32),
            vmem((2, nz - 1, nr, LANE), f32),
            vmem((2, nr, LANE), bf),
            vmem((2, 256, LANE), bf),
            vmem((2, 256, LANE), f32),
            vmem((STEPS * PANEL, LANE), f32),
            vmem((STEPS, 8, TILE, LANE), bf),
            dma((3,)), dma((npc,)), dma((npc,)), dma((npc,)), dma((2,)),
            dma((tb,)), dma((tb,)), dma((ta,)), dma((ta,)),
            dma((tb,)), dma((tb,)), dma((ta,)), dma((ta,)),
            dma((2, 4)), dma((3,)),
        ],
        compiler_params=pltpu.CompilerParams(
            collective_id=0, has_side_effects=True, vmem_limit_bytes=60 * 1024 * 1024),
    )(panel_ids, a_tile, b_tile, c_prior, sketch_matrix)


def solution(mesh):
    placed = (P("row", "col"), P("row", "col"), P("row", "col"), P("col", None), P())
    return jax.shard_map(
        functools.partial(per_device, mesh.shape["col"]),
        mesh=mesh,
        in_specs=placed,
        out_specs=(P("row", "col"), P("row", None), P("row", None)),
        check_vma=False,
    )
```

```python
import functools

import jax
import jax.numpy as jnp
from jax import lax
from jax.experimental import pallas as pl
from jax.experimental.pallas import tpu as pltpu
from jax.sharding import PartitionSpec as P

PANEL = 512
STEPS = 2
NX = 4
NY = 4
LANE = 128
PART = 128
TILE = 16
DELAY_A = 4
DELAY_B = 5
PIECES = ((0, 2), (2, 6), (6, 13))
MESH = pl.DeviceIdType.MESH


def kernel(dims, ids, a_hbm, b_hbm, c_hbm, s_hbm, cout_hbm, sk_hbm, pr_hbm,
           ab_v, bo_v, bp_v, c_v, s_v, sb, sa, rb, ra, afull, bfull, cov,
           part, rsr, red, outg, outb, bs, masks,
           in_sem, bo_sem, bp_send, bp_recv, ap_sem,
           sb_sem, rb_sem, sa_sem, ra_sem, fb_send, fb_recv, fa_send, fa_recv,
           rs_sem, out_sem):
    nz, na, nb, ta, tb, rows_k = dims
    r = lax.axis_index("row")
    z = lax.axis_index("col")
    core = lax.rem(r, 2)
    chip = r // 2
    x = lax.rem(chip, NX)
    y = chip // NX
    first_core = core == 0
    second_core = core == 1

    def at_chip(yy, xx):
        return (lax.rem(yy + NY, NY) * NX + lax.rem(xx + NX, NX)) * 2 + core

    partner = (chip * 2 + (1 - core), z)
    plane = ((at_chip(y, x + 1), z), (at_chip(y, x - 1), z),
             (at_chip(y + 1, x), z), (at_chip(y - 1, x), z))
    line = ((r, lax.rem(z + 1, nz)), (r, lax.rem(z + nz - 1, nz)))

    def piece(j):
        low, high = PIECES[j]
        return pl.ds(low * LANE, (high - low) * LANE)

    def own_load(j):
        return pltpu.make_async_copy(b_hbm.at[:, piece(j)], bo_v.at[:, piece(j)], bo_sem.at[j])

    def partner_copy(j):
        return pltpu.make_async_remote_copy(
            src_ref=bo_v.at[:, piece(j)], dst_ref=bp_v.at[:, piece(j)],
            send_sem=bp_send.at[j], recv_sem=bp_recv.at[j],
            device_id=partner, device_id_type=MESH)

    load_a = pltpu.make_async_copy(a_hbm, ab_v.at[core], in_sem.at[0])
    load_c = pltpu.make_async_copy(c_hbm, c_v, in_sem.at[1])
    load_s = pltpu.make_async_copy(s_hbm, s_v, in_sem.at[2])
    partner_a = pltpu.make_async_remote_copy(
        src_ref=ab_v.at[0], dst_ref=ab_v.at[0], send_sem=ap_sem.at[0], recv_sem=ap_sem.at[1],
        device_id=partner, device_id_type=MESH)
    npc = len(PIECES)

    barrier = pltpu.get_barrier_semaphore()
    pl.semaphore_signal(barrier, inc=1, device_id=partner, device_id_type=MESH)

    @pl.when(first_core)
    def _():
        for target in plane:
            pl.semaphore_signal(barrier, inc=1, device_id=target, device_id_type=MESH)

    @pl.when(second_core)
    def _():
        for target in line:
            pl.semaphore_signal(barrier, inc=1, device_id=target, device_id_type=MESH)

    load_a.start()
    for j in range(npc):
        own_load(j).start()

    def flag(cond):
        return cond.astype(jnp.int32)

    def choose(cond, one, two):
        return two + cond * (one - two)

    def within(v, low, high):
        return flag(v >= low) * flag(v <= high)

    pid = [ids[s] for s in range(STEPS)]
    owner_core = [lax.rem(p, 2) for p in pid]
    ox = [lax.rem(lax.div(p, 2), NX) for p in pid]
    oy = [lax.div(p, 2 * NX) for p in pid]
    oz = [lax.div(p * PANEL, rows_k) for p in pid]
    oa = [lax.rem(p * PANEL, rows_k) for p in pid]
    dx = [[lax.rem(g * (x - o) + NX, NX) for o in ox] for g in (1, -1)]
    dy = [[lax.rem(g * (y - o) + NY, NY) for o in oy] for g in (1, -1)]
    for s in range(STEPS):
        flags = (
            flag(owner_core[s] == core), flag(dx[0][s] == 0) * flag(dy[0][s] == 0),
            within(dx[0][s], 1, NX - 2), within(dx[1][s], 1, NX - 2),
            within(dy[0][s], 1, NY - 2), within(dy[1][s], 1, NY - 2),
            flag(oz[s] == z), flag(oa[s] > 0),
        )
        for n, f in enumerate(flags):
            masks[s, n] = jnp.full((TILE, LANE), f.astype(jnp.float32)).astype(jnp.bfloat16)
    HERE, ROOT, KEEP, ZROOT, HIGH = 0, 1, 2, 6, 7

    def pick(s, n, one, two):
        keep = jnp.concatenate([masks[s, n]] * (PART // TILE), axis=0) > 0
        return jnp.where(keep, one, two)

    def lanes(k):
        return pl.ds(pl.multiple_of(k * LANE, LANE), LANE)

    def own_b(s, k, base):
        rows = pl.ds(pl.multiple_of(base, PART), PART)
        return pick(s, HERE, bo_v[rows, lanes(k)], bp_v[rows, lanes(k)])

    def own_a(s, f, tile, j):
        rows = pl.ds(pl.multiple_of(j * PART, PART), PART)
        return pick(s, HIGH, ab_v[tile, rows, lanes(PANEL // LANE + f)], ab_v[tile, rows, lanes(f)])

    def send_b(t, link):
        return pltpu.make_async_remote_copy(
            src_ref=sb.at[t, link], dst_ref=rb.at[t, link],
            send_sem=sb_sem.at[t], recv_sem=rb_sem.at[t],
            device_id=plane[link], device_id_type=MESH)

    def send_a(t, link, src):
        return pltpu.make_async_remote_copy(
            src_ref=src, dst_ref=ra.at[t, link],
            send_sem=sa_sem.at[t], recv_sem=ra_sem.at[t],
            device_id=line[link], device_id_type=MESH)

    def share_b(t):
        return pltpu.make_async_remote_copy(
            src_ref=rb.at[t], dst_ref=rb.at[t],
            send_sem=fb_send.at[t], recv_sem=fb_recv.at[t],
            device_id=partner, device_id_type=MESH)

    def share_a(t):
        return pltpu.make_async_remote_copy(
            src_ref=ra.at[t], dst_ref=ra.at[t],
            send_sem=fa_send.at[t], recv_sem=fa_recv.at[t],
            device_id=partner, device_id_type=MESH)

    def wait_all(ref, sem):
        pltpu.make_async_copy(ref, ref, sem).wait()

    def stage_b(t, own, relay):
        for link, sign in ((0, 0), (1, 1), (2, 0), (3, 1)):
            mate = (link + 2) % 4
            q = link // 2
            for s in range(STEPS):
                rows = pl.ds(s * PART, PART)
                value = None
                if relay:
                    value = pick(s, KEEP + link, rb[t - DELAY_B, link, rows, :],
                                 rb[t - DELAY_B, mate, rows, :])
                if own:
                    mine = own_b(s, t, sign * (PANEL // 2) + q * PART)
                    value = pick(s, ROOT, mine, value) if relay else mine
                sb[t, link, rows, :] = value
            send_b(t, link).start()

    def stage_a(t, relay):
        for s in range(STEPS):
            rows = pl.ds(s * PART, PART)
            value = own_a(s, t // 4, lax.rem(t, 4) // 2, lax.rem(t, 2))
            for link in range(2):
                sa[t, link, rows, :] = (
                    pick(s, ZROOT, value, ra[t - DELAY_A, link, rows, :]) if relay else value)
        for link in range(2):
            send_a(t, link, sa.at[t, link]).start()

    @pl.when(first_core)
    def _():
        load_a.wait()
        pl.semaphore_wait(barrier, 5)
        partner_a.start()
        for t in range(DELAY_B):
            for j, (low, _) in enumerate(PIECES):
                if low == t:
                    own_load(j).wait()
                    partner_copy(j).start()
                    partner_copy(j).wait_recv()
            stage_b(t, True, False)
        load_c.start()
        load_s.start()

        def begin(t, carry):
            for j, (low, _) in enumerate(PIECES):
                if low >= DELAY_B:
                    @pl.when(t == low)
                    def _(j=j):
                        own_load(j).wait()
                        partner_copy(j).start()
                        partner_copy(j).wait_recv()

            wait_all(rb.at[t - DELAY_B], rb_sem.at[t - DELAY_B])
            stage_b(t, True, True)
            share_b(t - DELAY_B).start()
            return carry

        def relay(t, carry):
            wait_all(rb.at[t - DELAY_B], rb_sem.at[t - DELAY_B])
            stage_b(t, False, True)
            share_b(t - DELAY_B).start()
            return carry

        def last(t, carry):
            wait_all(rb.at[t], rb_sem.at[t])
            share_b(t).start()
            return carry

        lax.fori_loop(DELAY_B, nb, begin, 0)
        lax.fori_loop(nb, tb, relay, 0)
        lax.fori_loop(tb - DELAY_B, tb, last, 0)

    @pl.when(second_core)
    def _():
        pl.semaphore_wait(barrier, 3)
        for j in range(npc):
            own_load(j).wait()
            partner_copy(j).start()
        load_a.wait()
        partner_a.wait_recv()
        for t in range(DELAY_A):
            stage_a(t, False)
        load_c.start()
        load_s.start()

        def begin(t, carry):
            wait_all(ra.at[t - DELAY_A], ra_sem.at[t - DELAY_A])
            stage_a(t, True)
            share_a(t - DELAY_A).start()
            return carry

        def relay(t, carry):
            wait_all(ra.at[t - DELAY_A], ra_sem.at[t - DELAY_A])
            for link in range(2):
                send_a(t, link, ra.at[t - DELAY_A, link]).start()
            share_a(t - DELAY_A).start()
            return carry

        def last(t, carry):
            wait_all(ra.at[t], ra_sem.at[t])
            share_a(t).start()
            return carry

        lax.fori_loop(DELAY_A, na, begin, 0)
        lax.fori_loop(na, ta, relay, 0)
        lax.fori_loop(ta - DELAY_A, ta, last, 0)
        for j in range(npc):
            partner_copy(j).wait_recv()

        def settle(t, carry):
            wait_all(rb.at[t], fb_recv.at[t])
            return carry

        lax.fori_loop(0, tb, settle, 0)

    load_c.wait()
    load_s.wait()

    routes = []
    for s in range(STEPS):
        for g in range(2):
            i, j = dx[g][s], dy[g][s]
            i0, j0 = flag(i == 0), flag(j == 0)
            near = i0 + j0 - i0 * j0
            tx = (i + j + NX * i0 * (1 - j0) - 1 + i0 * j0) * DELAY_B
            ty = (i + j + NY * j0 * (1 - i0) - 1 + i0 * j0) * DELAY_B
            routes.append((s, g, 0, g + 2 * (1 - near), choose(near, tx, ty)))
            routes.append((s, g, 1, g + 2 * near, choose(near, ty, tx)))

    def take_b(k, carry):
        for s, g, q, link, first in routes:
            base = g * (PANEL // 2) + q * PART
            got = rb[k + first, link, pl.ds(s * PART, PART), :]
            bfull[pl.ds(s * PANEL + base, PART), lanes(k)] = pick(s, ROOT, own_b(s, k, base), got)
        return carry

    lax.fori_loop(0, nb, take_b, 0)

    width = nb * LANE
    blocks = [pl.ds(at, min(256, width - at)) for at in range(0, width, 256)]
    bs[...] = jnp.zeros_like(bs)
    for cols in blocks:
        bs[...] += jnp.dot(bfull[:, cols], s_v[cols, :], preferred_element_type=jnp.float32)

    @pl.when(first_core)
    def _():
        def settle(t, carry):
            wait_all(ra.at[t], fa_recv.at[t])
            return carry

        lax.fori_loop(0, ta, settle, 0)

    for s in range(STEPS):
        hz = lax.rem(z - oz[s] + nz, nz)
        down = flag(hz > nz // 2)
        hop = choose(down, nz - hz, hz)
        first = (hop - 1 + flag(hop == 0)) * DELAY_A
        for f in range(PANEL // LANE):
            for j in range(2):
                got = ra[first + 4 * f + 2 * core + j, down, pl.ds(s * PART, PART), :]
                afull[pl.ds(j * PART, PART), pl.ds(s * PANEL + f * LANE, LANE)] = pick(
                    s, ZROOT, own_a(s, f, core, j), got)

    nr = 256 // nz

    def rows_of(j):
        return pl.ds(pl.multiple_of(j * nr, nr), nr)

    order = sorted(range(1, nz), key=lambda d: -min(d, nz - d))

    def scatter(n, d):
        to = lax.rem(z + d, nz)
        return pltpu.make_async_remote_copy(
            src_ref=part.at[n, rows_of(to), :], dst_ref=rsr.at[n, d - 1],
            send_sem=rs_sem.at[n, 0], recv_sem=rs_sem.at[n, 1],
            device_id=(r, to), device_id_type=MESH)

    def gather(n, d):
        to = lax.rem(z + d, nz)
        return pltpu.make_async_remote_copy(
            src_ref=red.at[n], dst_ref=outg.at[n, rows_of(z), :],
            send_sem=rs_sem.at[n, 2], recv_sem=rs_sem.at[n, 3],
            device_id=(r, to), device_id_type=MESH)

    def reduce(n):
        wait_all(rsr.at[n], rs_sem.at[n, 1])
        value = part[n, rows_of(z), :]
        for d in range(nz - 1):
            value = value + rsr[n, d]
        red[n] = value.astype(jnp.bfloat16)
        outg[n, rows_of(z), :] = value.astype(jnp.bfloat16)
        for d in order:
            gather(n, d).start()

    pr = jnp.zeros((256, LANE), jnp.float32)
    rest = bs[...]
    for _ in range(3):
        term = rest.astype(jnp.bfloat16)
        pr = pr + jnp.dot(afull[...], term, preferred_element_type=jnp.float32)
        rest = rest - term.astype(jnp.float32)
    part[1] = pr
    for d in order:
        scatter(1, d).start()
    sk = jnp.zeros((256, LANE), jnp.float32)
    for cols in blocks:
        acc = jnp.dot(afull[...], bfull[:, cols], preferred_element_type=jnp.float32)
        c_new = (c_v[:, cols].astype(jnp.float32) + acc).astype(jnp.bfloat16)
        cov[:, cols] = c_new
        sk = sk + jnp.dot(c_new, s_v[cols, :], preferred_element_type=jnp.float32)
    part[0] = sk
    for d in order:
        scatter(0, d).start()
    put_c = pltpu.make_async_copy(cov, cout_hbm, out_sem.at[0])
    put_c.start()
    reduce(1)
    reduce(0)

    @pl.when(first_core)
    def _():
        def drain(t, carry):
            wait_all(sb.at[t], sb_sem.at[t])
            share_b(t).wait_send()
            return carry

        lax.fori_loop(0, tb, drain, 0)
        partner_a.wait_send()

    @pl.when(second_core)
    def _():
        def drain(t, carry):
            wait_all(sa.at[0], sa_sem.at[t])
            share_a(t).wait_send()
            return carry

        lax.fori_loop(0, ta, drain, 0)

    for j in range(npc):
        partner_copy(j).wait_send()
    wait_all(rsr.at[1], rs_sem.at[1, 0])
    wait_all(rsr.at[0], rs_sem.at[0, 0])
    others = pl.ds(0, 256 - nr)
    wait_all(outg.at[1, others], rs_sem.at[1, 2])
    put_c.wait()
    wait_all(outg.at[1, others], rs_sem.at[1, 3])
    outb[1] = outg[1].astype(jnp.float32)
    put_p = pltpu.make_async_copy(outb.at[1], pr_hbm, out_sem.at[2])
    put_p.start()
    wait_all(outg.at[0, others], rs_sem.at[0, 3])
    outb[0] = outg[0].astype(jnp.float32)
    put_s = pltpu.make_async_copy(outb.at[0], sk_hbm, out_sem.at[1])
    put_s.start()
    wait_all(outg.at[0, others], rs_sem.at[0, 2])
    put_s.wait()
    put_p.wait()


def finish(*refs):
    ins, outs, held, sems = refs[:3], refs[3:6], refs[6:9], refs[9]
    loads = [pltpu.make_async_copy(i, h, sems.at[0, n]) for n, (i, h) in enumerate(zip(ins, held))]
    stores = [pltpu.make_async_copy(h, o, sems.at[1, n]) for n, (h, o) in enumerate(zip(held, outs))]
    for load in loads:
        load.start()
    for load, store in zip(loads, stores):
        load.wait()
        store.start()
    for store in stores:
        store.wait()


def per_device(nz, a_tile, b_tile, c_prior, sketch_matrix, panel_ids):
    width = b_tile.shape[1]
    nb = width // LANE
    rows_k = a_tile.shape[1]
    na = (PANEL // LANE) * (2 * 256 // PART)
    tb = nb + 6 * DELAY_B
    ta = na + (nz // 2 - 1) * DELAY_A
    bf = jnp.bfloat16
    f32 = jnp.float32
    dma = pltpu.SemaphoreType.DMA
    vmem = pltpu.VMEM
    nr = 256 // nz
    npc = len(PIECES)
    hbm = pl.BlockSpec(memory_space=pl.ANY)
    results = pl.pallas_call(
        functools.partial(kernel, (nz, na, nb, ta, tb, rows_k)),
        out_shape=(
            jax.ShapeDtypeStruct((256, width), bf),
            jax.ShapeDtypeStruct((256, LANE), f32),
            jax.ShapeDtypeStruct((256, LANE), f32),
        ),
        in_specs=[pl.BlockSpec(memory_space=pltpu.SMEM)] + [hbm] * 4,
        out_specs=(hbm,) * 3,
        scratch_shapes=[
            vmem((2, 256, rows_k), bf),
            vmem((PANEL, width), bf),
            vmem((PANEL, width), bf),
            vmem((256, width), bf),
            vmem((width, LANE), bf),
            vmem((tb, 4, STEPS * PART, LANE), bf),
            vmem((na, 2, STEPS * PART, LANE), bf),
            vmem((tb, 4, STEPS * PART, LANE), bf),
            vmem((ta, 2, STEPS * PART, LANE), bf),
            vmem((256, STEPS * PANEL), bf),
            vmem((STEPS * PANEL, width), bf),
            vmem((256, width), bf),
            vmem((2, 256, LANE), f32),
            vmem((2, nz - 1, nr, LANE), f32),
            vmem((2, nr, LANE), bf),
            vmem((2, 256, LANE), bf),
            vmem((2, 256, LANE), f32),
            vmem((STEPS * PANEL, LANE), f32),
            vmem((STEPS, 8, TILE, LANE), bf),
            dma((3,)), dma((npc,)), dma((npc,)), dma((npc,)), dma((2,)),
            dma((tb,)), dma((tb,)), dma((ta,)), dma((ta,)),
            dma((tb,)), dma((tb,)), dma((ta,)), dma((ta,)),
            dma((2, 4)), dma((3,)),
        ],
        compiler_params=pltpu.CompilerParams(
            collective_id=0, has_side_effects=True, vmem_limit_bytes=60 * 1024 * 1024),
    )(panel_ids, a_tile, b_tile, c_prior, sketch_matrix)
    return pl.pallas_call(
        finish,
        out_shape=tuple(jax.ShapeDtypeStruct(v.shape, v.dtype) for v in results),
        in_specs=[hbm] * 3,
        out_specs=(hbm,) * 3,
        scratch_shapes=[vmem(v.shape, v.dtype) for v in results] + [dma((2, 3))],
    )(*results)


def solution(mesh):
    placed = (P("row", "col"), P("row", "col"), P("row", "col"), P("col", None), P())
    return jax.shard_map(
        functools.partial(per_device, mesh.shape["col"]),
        mesh=mesh,
        in_specs=placed,
        out_specs=(P("row", "col"), P("row", None), P("row", None)),
        check_vma=False,
    )
```
